256 devices in a mesh: dp: 2 (over y_hi), expert: 128 (over x, y_lo, z, core).
Axes of the slice: x: 4, y: 4 (y_hi: 2, y_lo: 2; y = y_hi * 2 + y_lo), z: 8, core: 2. Of those that a mesh axis runs over, the one named last changes fastest.
Arguments:
- tokens: bfloat16 [4096, 4096], P(('dp', 'expert')), may hold values from -6 to 6
- routing: int32 [4096, 2], P(('dp', 'expert')), may hold values from 0 to 7, as said below
- hidden_grad: bfloat16 [131072, 512], P(('dp', 'expert')), may hold values from -3 to 3
- gate_weight: bfloat16 [4096, 65536], P(None, 'expert'), may hold values from -0.09375 to 0.09375
- up_weight: bfloat16 [4096, 65536], P(None, 'expert'), may hold values from -0.09375 to 0.09375
Outputs:
- token_grad: bfloat16 [4096, 4096], P(('dp', 'expert'))
- gate_weight_grad: bfloat16 [4096, 65536], P('dp', 'expert')
- up_weight_grad: bfloat16 [4096, 65536], P('dp', 'expert')
The draws below stay inside these ranges and needn't reach their ends.
Inputs may be any that keep to these rules, and one draw needn't show every extreme that they name: `routing`: the 2 entries of a token differ, and no device names one expert in more than 4 of its tokens.
All inputs are finite; a program needn't handle non-finite values.
Results may differ from the reference program's by a relative error of at most 0.0085.
Values may be sent and summed in bfloat16 or wider, within the bound.
No kernel may reach another device: no remote copies, remote signals or barrier semaphores. Data moves between devices by JAX's collectives and lax.ppermute only.
A program may use at most 128 MiB of HBM per device.

```python
import jax
import jax.numpy as jnp
from jax import lax

D = 4096
EXPERTS = 8
TOP = 2
FF = 8192
CAP = 4
TOK = 16
FFD = 512
ROWS = 512
TOKENS = 4096
N_DP = 2
N_EXPERT = 128
DEVICES = 256


def draw_routing(key, part):
    hot_expert = jax.random.randint(jax.random.fold_in(key, 11), (), 0, EXPERTS)
    block_keys = jax.random.split(jax.random.fold_in(key, 12), TOKENS // TOK)

    def one_block(block_key):
        key_order, key_cycle, key_offset, key_flip = jax.random.split(block_key, 4)
        order = jax.random.permutation(key_order, TOK)
        token_rank = jnp.argsort(order, stable=True).astype(jnp.int32)
        cycle = jax.random.permutation(key_cycle, EXPERTS - 1).astype(jnp.int32)
        offset = jax.random.randint(key_offset, (), 0, EXPERTS - 1)
        flipped = jax.random.randint(key_flip, (TOK,), 0, 2)
        first_index = token_rank + jnp.maximum(token_rank - CAP, 0)

        def other_expert(index):
            return (hot_expert + 1 + cycle[(index + offset) % (EXPERTS - 1)]) % EXPERTS
        first_other = other_expert(first_index)
        second_other = other_expert(first_index + 1)
        is_hot = token_rank < CAP
        column_a = jnp.where(is_hot, jnp.where(flipped == 1, hot_expert, first_other), first_other)
        column_b = jnp.where(is_hot, jnp.where(flipped == 1, first_other, hot_expert), second_other)
        return jnp.stack([column_a, column_b], axis=1)
    return jax.vmap(one_block)(block_keys).reshape(TOKENS, TOP).astype(jnp.int32)


def level_of(own_key, extent, cuts, least, top_value):
    gain = 1.0
    for axis_at, shards_of in cuts:
        steps = jax.random.uniform(jax.random.fold_in(jax.random.fold_in(own_key, 6), axis_at), (shards_of,), jnp.float32, least / len(cuts), top_value / len(cuts))
        gain = gain * jnp.repeat(jnp.exp(steps), extent[axis_at] // shards_of).reshape((-1,) + (1,) * (len(extent) - 1 - axis_at))
    return gain


def normal_values(rng, dims, deviation, limit, pieces=(), held_as=jnp.bfloat16):
    values = jax.random.normal(rng, dims, jnp.float32) * deviation
    if len(pieces) > 0:
        values = level_of(rng, dims, pieces, -0.22, 0.18) * values
    return jnp.clip(values, min=-limit, max=limit).astype(held_as)


def setup_inputs(seed: int = 0) -> dict:
    arg_keys = jax.random.split(jax.random.key(seed), 6)
    tokens = normal_values(arg_keys[0], (TOKENS, D), 1.0, 6.0, ((0, 256),))
    routing = draw_routing(jax.random.fold_in(arg_keys[5], 71), 0)
    hidden_grad = normal_values(arg_keys[2], (DEVICES * ROWS, FFD), 0.5, 3.0, ((0, 256),))
    gate_weight = normal_values(arg_keys[3], (D, EXPERTS * FF), D ** -0.5, 0.09375, ((1, 128),))
    up_weight = normal_values(arg_keys[4], (D, EXPERTS * FF), D ** -0.5, 0.09375, ((1, 128),))
    return dict(tokens=tokens, routing=routing, hidden_grad=hidden_grad, gate_weight=gate_weight, up_weight=up_weight)


def slot_tables(routing_dev):
    flat_experts = routing_dev.reshape(-1)
    onehot = (flat_experts[:, None] == jnp.arange(EXPERTS, dtype=jnp.int32)[None, :]).astype(jnp.int32)
    before = jnp.cumsum(onehot, axis=0) - onehot
    slot_index = jnp.sum(before * onehot, axis=1)
    target = flat_experts * CAP + slot_index
    placed = target[:, None] == jnp.arange(EXPERTS * CAP, dtype=jnp.int32)[None, :]
    return placed.astype(jnp.float32)


def reference(tokens, routing, hidden_grad, gate_weight, up_weight):
    shards = N_EXPERT // EXPERTS
    ffd_cols = FF // shards
    row_count = N_EXPERT * CAP
    token_blocks = tokens.reshape(N_DP, N_EXPERT, TOK, D)
    route_blocks = routing.reshape(N_DP, N_EXPERT, TOK, TOP)
    placed = jax.vmap(jax.vmap(slot_tables))(route_blocks)
    doubled = jnp.repeat(token_blocks, TOP, axis=2).astype(jnp.float32)
    outgoing = jnp.einsum('rsae,rsad->rsed', placed, doubled, precision=lax.Precision.HIGHEST)
    outgoing = outgoing.astype(jnp.bfloat16).reshape(N_DP, N_EXPERT, EXPERTS, CAP, D)
    expert_inputs = outgoing.transpose(2, 0, 1, 3, 4).reshape(EXPERTS, N_DP, row_count, D)
    grad_blocks = hidden_grad.reshape(N_DP, EXPERTS, shards, row_count, ffd_cols).transpose(1, 0, 2, 3, 4)
    gate_blocks = gate_weight.reshape(D, EXPERTS, FF).transpose(1, 0, 2)
    up_blocks = up_weight.reshape(D, EXPERTS, FF).transpose(1, 0, 2)

    def one_expert(inputs):
        expert_x, expert_h, w_gate, w_up = inputs
        gate_total = jnp.zeros((D, FF), jnp.float32)
        up_total = jnp.zeros((D, FF), jnp.float32)
        sums = []
        for replica in range(N_DP):
            expert_rows = expert_x[replica]
            gate_pre = jnp.dot(expert_rows, w_gate, preferred_element_type=jnp.float32)
            up_pre = jnp.dot(expert_rows, w_up, preferred_element_type=jnp.float32)
            grad_h = expert_h[replica].transpose(1, 0, 2).reshape(row_count, FF).astype(jnp.float32)
            sigmoid_gate = jax.nn.sigmoid(gate_pre)
            gate_grad = (grad_h * up_pre * sigmoid_gate * (1.0 + gate_pre * (1.0 - sigmoid_gate))).astype(jnp.bfloat16)
            up_grad = (grad_h * gate_pre * sigmoid_gate).astype(jnp.bfloat16)
            first_part = jnp.einsum('rsf,dsf->srd', gate_grad.reshape(row_count, shards, ffd_cols).astype(jnp.float32),
                                    w_gate.reshape(D, shards, ffd_cols).astype(jnp.float32))
            second_part = jnp.einsum('rsf,dsf->srd', up_grad.reshape(row_count, shards, ffd_cols).astype(jnp.float32),
                                     w_up.reshape(D, shards, ffd_cols).astype(jnp.float32))
            partial_value = (first_part + second_part).astype(jnp.bfloat16).astype(jnp.float32)
            sums.append(jnp.sum(partial_value, axis=0))
            gate_term = jnp.dot(expert_rows.T, gate_grad, preferred_element_type=jnp.float32)
            up_term = jnp.dot(expert_rows.T, up_grad, preferred_element_type=jnp.float32)
            gate_total = gate_total + gate_term.astype(jnp.bfloat16).astype(jnp.float32)
            up_total = up_total + up_term.astype(jnp.bfloat16).astype(jnp.float32)
        return jnp.stack(sums), gate_total.astype(jnp.bfloat16), up_total.astype(jnp.bfloat16)

    partial_sums, gate_grads, up_grads = lax.map(one_expert, (expert_inputs, grad_blocks, gate_blocks, up_blocks))
    back = partial_sums.reshape(EXPERTS, N_DP, N_EXPERT, CAP, D).transpose(1, 2, 0, 3, 4)
    back = back.reshape(N_DP, N_EXPERT, EXPERTS * CAP, D)
    gathered = jnp.einsum('rsae,rsed->rsad', placed, back, precision=lax.Precision.HIGHEST)
    token_grad = jnp.sum(gathered.reshape(N_DP, N_EXPERT, TOK, TOP, D), axis=3).astype(jnp.bfloat16)
    token_grad = token_grad.reshape(TOKENS, D)
    gate_weight_grad = gate_grads.transpose(1, 0, 2).reshape(D, EXPERTS * FF)
    up_weight_grad = up_grads.transpose(1, 0, 2).reshape(D, EXPERTS * FF)
    return token_grad, gate_weight_grad, up_weight_grad
```

```python
import jax
import jax.numpy as jnp
from jax import lax
from jax.sharding import Mesh, PartitionSpec as P

EXPERTS = 8
TOP = 2
CAP = 4


def slot_tables(routing_dev):
    flat_experts = routing_dev.reshape(-1)
    onehot = (flat_experts[:, None] == jnp.arange(EXPERTS, dtype=jnp.int32)[None, :]).astype(
        jnp.int32
    )
    before = jnp.cumsum(onehot, axis=0) - onehot
    slot_index = jnp.sum(before * onehot, axis=1)
    target = flat_experts * CAP + slot_index
    placed = target[:, None] == jnp.arange(EXPERTS * CAP, dtype=jnp.int32)[None, :]
    return placed.astype(jnp.float32)


def contract_rows(left_rows, right_rows):
    return lax.dot_general(
        left_rows, right_rows, (((0,), (0,)), ((), ())), preferred_element_type=jnp.float32
    )


def swap_dp(block):
    return lax.ppermute(block, "dp", [(0, 1), (1, 0)])


def per_device(tokens, routing, hidden_grad, gate_weight, up_weight):
    token_count, model_width = tokens.shape
    ffd = gate_weight.shape[1]
    shards = lax.axis_size("s")
    half = model_width // 2
    replica = lax.axis_index("dp")
    placed = slot_tables(routing)
    chosen = jnp.sum(placed.reshape(token_count, TOP, EXPERTS * CAP), axis=1)
    outgoing = lax.dot_general(
        chosen.astype(jnp.bfloat16), tokens, (((0,), (0,)), ((), ())),
        preferred_element_type=jnp.float32,
    ).astype(jnp.bfloat16)
    mine = lax.all_to_all(
        outgoing.reshape(EXPERTS, CAP, model_width), "e", split_axis=0, concat_axis=0, tiled=True
    ).reshape(EXPERTS * CAP, model_width)
    far_mine = swap_dp(lax.dynamic_slice_in_dim(mine, (1 - replica) * half, half, 1))
    rows = lax.all_gather(mine, "s", axis=0, tiled=True)
    far_rows = lax.all_gather(far_mine, "s", axis=0, tiled=True)
    grad_h = (
        hidden_grad.reshape(EXPERTS, shards, CAP, ffd)
        .transpose(1, 0, 2, 3)
        .reshape(-1, ffd)
        .astype(jnp.float32)
    )
    gate_pre = jnp.dot(rows, gate_weight, preferred_element_type=jnp.float32)
    up_pre = jnp.dot(rows, up_weight, preferred_element_type=jnp.float32)
    sig = jax.nn.sigmoid(gate_pre)
    gate_grad = (grad_h * up_pre * sig * (1.0 + gate_pre * (1.0 - sig))).astype(jnp.bfloat16)
    up_grad = (grad_h * gate_pre * sig).astype(jnp.bfloat16)
    grads = jnp.concatenate([gate_grad, up_grad], axis=1)
    far_grads = swap_dp(grads)
    transposed = (((1,), (1,)), ((), ()))
    partial_value = lax.dot_general(
        gate_grad, gate_weight, transposed, preferred_element_type=jnp.float32
    )
    partial_value = partial_value + lax.dot_general(
        up_grad, up_weight, transposed, preferred_element_type=jnp.float32
    )
    partial_value = partial_value.astype(jnp.bfloat16)
    summed = lax.psum_scatter(partial_value, "s", scatter_dimension=0, tiled=True)
    back = lax.all_to_all(
        summed.reshape(EXPERTS, CAP, model_width), "e", split_axis=0, concat_axis=0, tiled=True
    ).reshape(EXPERTS * CAP, model_width)
    token_grad = jnp.dot(
        chosen.astype(jnp.bfloat16), back, preferred_element_type=jnp.float32
    ).astype(jnp.bfloat16)
    own_columns = lax.dynamic_slice_in_dim(rows, replica * half, half, 1)
    own_term = lax.optimization_barrier(contract_rows(own_columns, grads).astype(jnp.bfloat16))
    weight_sum = own_term.astype(jnp.float32) + contract_rows(far_rows, far_grads)
    return (
        token_grad,
        weight_sum[:, :ffd].astype(jnp.bfloat16),
        weight_sum[:, ffd:].astype(jnp.bfloat16),
    )


def solution(mesh):
    n_dp, n_expert = mesh.devices.shape
    fine = Mesh(mesh.devices.reshape(n_dp, EXPERTS, n_expert // EXPERTS), ("dp", "e", "s"))
    all_axes = ("dp", "e", "s")
    in_specs = (
        P(all_axes, None),
        P(all_axes, None),
        P(all_axes, None),
        P(None, ("e", "s")),
        P(None, ("e", "s")),
    )
    out_specs = (P(all_axes, None), P("dp", ("e", "s")), P("dp", ("e", "s")))
    return jax.shard_map(
        per_device, mesh=fine, in_specs=in_specs, out_specs=out_specs, check_vma=False
    )
```

```python
import jax
import jax.numpy as jnp
from jax import lax
from jax.sharding import Mesh, PartitionSpec as P

EXPERTS = 8
TOP = 2
CAP = 4
CORES = 2


def slot_tables(routing_dev):
    flat_experts = routing_dev.reshape(-1)
    onehot = (flat_experts[:, None] == jnp.arange(EXPERTS, dtype=jnp.int32)[None, :]).astype(
        jnp.int32
    )
    before = jnp.cumsum(onehot, axis=0) - onehot
    slot_index = jnp.sum(before * onehot, axis=1)
    target = flat_experts * CAP + slot_index
    placed = target[:, None] == jnp.arange(EXPERTS * CAP, dtype=jnp.int32)[None, :]
    return placed.astype(jnp.float32)


def contract_rows(left_rows, right_rows):
    return lax.dot_general(
        left_rows, right_rows, (((0,), (0,)), ((), ())), preferred_element_type=jnp.float32
    )


def swap_dp(block):
    return lax.ppermute(block, "dp", [(0, 1), (1, 0)])


def swap_core(block):
    return lax.ppermute(block, "c", [(0, 1), (1, 0)])


def ring(block):
    count = lax.axis_size("z")
    route = []
    for at in range(count):
        route.append((at * CORES, (at + 1) % count * CORES))
        route.append((at * CORES + 1, (at - 1) % count * CORES + 1))
    return lax.ppermute(block, ("z", "c"), route)


def per_device(tokens, routing, hidden_grad, gate_weight, up_weight):
    token_count, model_width = tokens.shape
    ffd = gate_weight.shape[1]
    chips = lax.axis_size("z")
    rounds = chips // 2
    half = model_width // 2
    chunk = EXPERTS * CAP
    replica = lax.axis_index("dp")
    core = lax.axis_index("c")
    at = lax.axis_index("z")

    placed = slot_tables(routing)
    chosen = jnp.sum(placed.reshape(token_count, TOP, chunk), axis=1).astype(jnp.bfloat16)
    outgoing = contract_rows(chosen, tokens).astype(jnp.bfloat16)
    mine = lax.all_to_all(
        outgoing.reshape(EXPERTS, CAP, model_width), "e", split_axis=0, concat_axis=0, tiled=True
    ).reshape(chunk, model_width)

    by_chip = hidden_grad.reshape(EXPERTS, chips, CORES, CAP, ffd).transpose(1, 2, 0, 3, 4)
    by_chip = by_chip.reshape(chips, CORES, chunk, ffd)
    by_chip = jnp.where(core == 0, by_chip, by_chip[:, ::-1])
    step = jnp.where(core == 0, -1, 1)

    def grad_rows(k):
        near = lax.dynamic_index_in_dim(by_chip, (at + step * k) % chips, 0, keepdims=False)
        far = lax.dynamic_index_in_dim(by_chip, (at - step * k) % chips, 0, keepdims=False)
        if k == 0:
            return near.reshape(CORES * chunk, ffd)
        if k == rounds:
            return near.reshape(CORES * chunk, ffd)
        return jnp.concatenate([near[0], near[1], far[1], far[0]], axis=0)

    transposed = (((1,), (1,)), ((), ()))

    def expert_grads(rows, k):
        grad_h = grad_rows(k).astype(jnp.float32)
        gate_pre = jnp.dot(rows, gate_weight, preferred_element_type=jnp.float32)
        up_pre = jnp.dot(rows, up_weight, preferred_element_type=jnp.float32)
        sig = jax.nn.sigmoid(gate_pre)
        gate_grad = (grad_h * up_pre * sig * (1.0 + gate_pre * (1.0 - sig))).astype(jnp.bfloat16)
        up_grad = (grad_h * gate_pre * sig).astype(jnp.bfloat16)
        partial_value = lax.dot_general(
            gate_grad, gate_weight, transposed, preferred_element_type=jnp.float32
        ) + lax.dot_general(up_grad, up_weight, transposed, preferred_element_type=jnp.float32)
        return jnp.concatenate([gate_grad, up_grad], axis=1), partial_value.astype(jnp.bfloat16)

    def far_half(block):
        return lax.dynamic_slice_in_dim(block, (1 - replica) * half, half, 1)

    native = [mine]
    other = [swap_core(mine)]
    travelling = jnp.concatenate([mine, other[0]], axis=0)
    for k in range(1, rounds + 1):
        travelling = ring(travelling if k < rounds else travelling[:chunk])
        native.append(travelling)
        other.append(swap_core(travelling))
    rows, grads, partials = [], [], []
    for k in range(rounds + 1):
        block = jnp.concatenate([native[k], other[k]], axis=0)
        grad, partial_value = expert_grads(block, k)
        rows.append(block)
        grads.append(grad)
        partials.append(partial_value)

    early = swap_dp(far_half(jnp.concatenate(native[: rounds - 1], axis=0)))
    late = swap_dp(far_half(jnp.concatenate(native[rounds - 1 :], axis=0)))
    far_native = jnp.concatenate([early, late], axis=0)
    far_other = swap_core(far_native)
    far_blocks = []
    start = 0
    for k in range(rounds + 1):
        size = native[k].shape[0]
        far_blocks += [far_native[start : start + size], far_other[start : start + size]]
        start += size
    far_rows = jnp.concatenate(far_blocks, axis=0)
    far_grads = jnp.concatenate(
        [
            swap_dp(jnp.concatenate(grads[: rounds - 1], axis=0)),
            swap_dp(jnp.concatenate(grads[rounds - 1 :], axis=0)),
        ],
        axis=0,
    )

    def chip_sum(k):
        size = native[k].shape[0]
        given = swap_core(partials[k][:size])
        return partials[k][size:].astype(jnp.float32) + given.astype(jnp.float32)

    total = chip_sum(rounds).astype(jnp.bfloat16)
    for k in range(rounds - 1, 0, -1):
        arrived = ring(total).astype(jnp.float32)
        if arrived.shape[0] < CORES * chunk:
            arrived = jnp.pad(arrived, ((0, CORES * chunk - arrived.shape[0]), (0, 0)))
        total = (chip_sum(k) + arrived).astype(jnp.bfloat16)
    arrived = ring(total).astype(jnp.float32)
    own = partials[0].astype(jnp.float32)
    given = swap_core((arrived[:chunk] + own[chunk:]).astype(jnp.bfloat16))
    summed = (given.astype(jnp.float32) + arrived[chunk:] + own[:chunk]).astype(jnp.bfloat16)
    back = lax.all_to_all(
        summed.reshape(EXPERTS, CAP, model_width), "e", split_axis=0, concat_axis=0, tiled=True
    ).reshape(chunk, model_width)
    token_grad = jnp.dot(chosen, back, preferred_element_type=jnp.float32).astype(jnp.bfloat16)

    own_columns = jnp.concatenate(
        [lax.dynamic_slice_in_dim(block, replica * half, half, 1) for block in rows], axis=0
    )
    own_term = contract_rows(own_columns, jnp.concatenate(grads, axis=0)).astype(jnp.bfloat16)
    own_term = lax.optimization_barrier(own_term)
    weight_sum = own_term.astype(jnp.float32) + contract_rows(far_rows, far_grads)
    return (
        token_grad,
        weight_sum[:, :ffd].astype(jnp.bfloat16),
        weight_sum[:, ffd:].astype(jnp.bfloat16),
    )


def solution(mesh):
    n_dp, n_expert = mesh.devices.shape
    chips = n_expert // EXPERTS // CORES
    fine = Mesh(mesh.devices.reshape(n_dp, EXPERTS, chips, CORES), ("dp", "e", "z", "c"))
    expert = ("e", "z", "c")
    tokenwise = P(("dp",) + expert, None)
    in_specs = (tokenwise, tokenwise, tokenwise, P(None, expert), P(None, expert))
    out_specs = (tokenwise, P("dp", expert), P("dp", expert))
    return jax.shard_map(
        per_device, mesh=fine, in_specs=in_specs, out_specs=out_specs, check_vma=False
    )
```

```python
import jax
import jax.numpy as jnp
from jax import lax
from jax.sharding import Mesh, PartitionSpec as P


EXPERTS = 8
TOP = 2
CAP = 4
CORES = 2


def slot_tables(routing_dev):
    flat_experts = routing_dev.reshape(-1)
    onehot = (flat_experts[:, None] == jnp.arange(EXPERTS, dtype=jnp.int32)[None, :]).astype(
        jnp.int32
    )
    before = jnp.cumsum(onehot, axis=0) - onehot
    slot_index = jnp.sum(before * onehot, axis=1)
    target = flat_experts * CAP + slot_index
    placed = target[:, None] == jnp.arange(EXPERTS * CAP, dtype=jnp.int32)[None, :]
    return placed.astype(jnp.float32)


def contract_rows(left_rows, right_rows):
    return lax.dot_general(
        left_rows, right_rows, (((0,), (0,)), ((), ())), preferred_element_type=jnp.float32
    )


def swap_dp(block):
    return lax.ppermute(block, "dp", [(0, 1), (1, 0)])


def swap_core(block):
    return lax.ppermute(block, "c", [(0, 1), (1, 0)])


def ring(block):
    count = lax.axis_size("z")
    route = []
    for at in range(count):
        route.append((at * CORES, (at + 1) % count * CORES))
        route.append((at * CORES + 1, (at - 1) % count * CORES + 1))
    return lax.ppermute(block, ("z", "c"), route)


def device_step(tokens, routing, hidden_grad, gate_weight, up_weight):
    token_count, model_width = tokens.shape
    ffd = gate_weight.shape[1]
    chips = lax.axis_size("z")
    rounds = chips // 2
    half = model_width // 2
    chunk = EXPERTS * CAP
    replica = lax.axis_index("dp")
    core = lax.axis_index("c")
    at = lax.axis_index("z")

    placed = slot_tables(routing)
    chosen = jnp.sum(placed.reshape(token_count, TOP, chunk), axis=1).astype(jnp.bfloat16)
    outgoing = contract_rows(chosen, tokens).astype(jnp.bfloat16)
    mine = lax.all_to_all(
        outgoing.reshape(EXPERTS, CAP, model_width), "e", split_axis=0, concat_axis=0, tiled=True
    ).reshape(chunk, model_width)

    by_chip = hidden_grad.reshape(EXPERTS, chips, CORES, CAP, ffd).transpose(1, 2, 0, 3, 4)
    by_chip = by_chip.reshape(chips, CORES, chunk, ffd)
    by_chip = jnp.where(core == 0, by_chip, by_chip[:, ::-1])
    step = jnp.where(core == 0, -1, 1)

    def grad_rows(k):
        near = lax.dynamic_index_in_dim(by_chip, (at + step * k) % chips, 0, keepdims=False)
        far = lax.dynamic_index_in_dim(by_chip, (at - step * k) % chips, 0, keepdims=False)
        if k == 0 or k == rounds:
            return near.reshape(CORES * chunk, ffd)
        return jnp.concatenate([near[0], near[1], far[1], far[0]], axis=0)

    def expert_grads(rows, k):
        grad_h = grad_rows(k).astype(jnp.float32)
        gate_pre = jnp.dot(rows, gate_weight, preferred_element_type=jnp.float32)
        up_pre = jnp.dot(rows, up_weight, preferred_element_type=jnp.float32)
        sig = jax.nn.sigmoid(gate_pre)
        gate_grad = (grad_h * up_pre * sig * (1.0 + gate_pre * (1.0 - sig))).astype(jnp.bfloat16)
        up_grad = (grad_h * gate_pre * sig).astype(jnp.bfloat16)
        return lax.optimization_barrier((gate_grad, up_grad))

    def partial_of(pair):
        transposed = (((1,), (1,)), ((), ()))
        gate_part = lax.dot_general(
            pair[0], gate_weight, transposed, preferred_element_type=jnp.float32
        )
        up_part = lax.dot_general(
            pair[1], up_weight, transposed, preferred_element_type=jnp.float32
        )
        return lax.optimization_barrier((gate_part + up_part).astype(jnp.bfloat16))

    def far_half(blocks):
        block = jnp.concatenate(blocks, axis=0)
        return lax.dynamic_slice_in_dim(block, (1 - replica) * half, half, 1)

    other_mine = swap_core(mine)
    travelling = [mine, other_mine]
    native = [mine]
    other = [other_mine]
    for k in range(1, rounds + 1):
        moved = []
        for part in travelling if k < rounds else travelling[:1]:
            moved.append(ring(part))
        travelling = moved
        native.append(jnp.concatenate(travelling, axis=0))
        other.append(swap_core(native[k]))
    sizes = [part.shape[0] for part in native]
    grads = []
    for k in range(rounds + 1):
        block = lax.optimization_barrier(jnp.concatenate([native[k], other[k]], axis=0))
        grads.append(expert_grads(block, k))

    given, kept = [None] * (rounds + 1), [None] * (rounds + 1)

    def partial_group(members):
        pair = []
        for which in range(2):
            blocks = [grads[k][which][: sizes[k]] for k in members]
            blocks += [grads[k][which][sizes[k] :] for k in members]
            pair.append(jnp.concatenate(blocks, axis=0))
        product = partial_of(pair)
        count = sum(sizes[k] for k in members)
        skip = sizes[0] if members[0] == 0 else 0
        gift = swap_core(product[skip:count])
        start = 0
        for k in members:
            if k > 0:
                given[k] = gift[start - skip : start - skip + sizes[k]]
            else:
                given[k] = product[: sizes[k]]
            kept[k] = product[count + start : count + start + sizes[k]]
            start += sizes[k]

    partial_group([rounds - 1, rounds])
    partial_group(list(range(rounds - 1)))

    early = swap_dp(far_half(native[: rounds - 1]))
    early = jnp.concatenate([early, swap_dp(far_half(native[rounds - 1 : rounds]))], axis=0)
    early_other = swap_core(early)
    last = far_half(native[rounds:])
    by_kind = []
    for which in range(2):
        blocks = [pair[which][:size] for pair, size in zip(grads, sizes)]
        blocks += [pair[which][size:] for pair, size in zip(grads, sizes)]
        by_kind.append(jnp.concatenate(blocks, axis=0))
    own_grads = jnp.concatenate(by_kind, axis=1)
    row_count = own_grads.shape[0]
    packed = [own_grads] + [last[:, i : i + 2 * ffd] for i in range(0, half, 2 * ffd)]
    received = swap_dp(jnp.concatenate(packed, axis=0))
    far_grads = received[:row_count]
    late = [received[i : i + chunk] for i in range(row_count, received.shape[0], chunk)]
    late = jnp.concatenate(late, axis=1)
    late_other = swap_core(late)
    far_early = lax.optimization_barrier(jnp.concatenate([early, early_other], axis=0))
    count = early.shape[0]
    far_rows = jnp.concatenate([far_early[:count], late, far_early[count:], late_other], axis=0)

    arrived = []
    for k in range(rounds, 0, -1):
        total = []
        for i in range(sizes[k] // chunk):
            spot = slice(i * chunk, (i + 1) * chunk)
            keep, gift = kept[k][spot], given[k][spot]
            if i > 0:
                keep, gift, total[0] = lax.optimization_barrier((keep, gift, total[0]))
            value = keep.astype(jnp.float32) + gift.astype(jnp.float32)
            if i < len(arrived):
                value = value + arrived[i].astype(jnp.float32)
            total.append(lax.optimization_barrier(value.astype(jnp.bfloat16)))
        arrived = []
        for part in total:
            arrived.append(ring(part))
    arrived = [part.astype(jnp.float32) for part in arrived]
    gift = swap_core((arrived[0] + kept[0].astype(jnp.float32)).astype(jnp.bfloat16))
    summed = gift.astype(jnp.float32) + arrived[1] + given[0].astype(jnp.float32)
    summed = summed.astype(jnp.bfloat16)
    back = lax.all_to_all(
        summed.reshape(EXPERTS, CAP, model_width), "e", split_axis=0, concat_axis=0, tiled=True
    ).reshape(chunk, model_width)
    token_grad = jnp.dot(chosen, back, preferred_element_type=jnp.float32).astype(jnp.bfloat16)

    ordered = [part for part in native] + [part for part in other]
    own_columns = jnp.concatenate(
        [lax.dynamic_slice_in_dim(part, replica * half, half, 1) for part in ordered], axis=0
    )
    own_columns = lax.optimization_barrier(own_columns)
    own_term = contract_rows(own_columns, own_grads).astype(jnp.bfloat16)
    own_term = lax.optimization_barrier(own_term)

    def weight_grad(begin):
        far_term = contract_rows(far_rows, far_grads[:, begin : begin + ffd])
        own_part = own_term[:, begin : begin + ffd].astype(jnp.float32)
        return (own_part + far_term).astype(jnp.bfloat16)

    return (token_grad, weight_grad(0), weight_grad(ffd))


def solution(mesh):
    n_dp, n_expert = mesh.devices.shape
    chips = n_expert // EXPERTS // CORES
    fine = Mesh(mesh.devices.reshape(n_dp, EXPERTS, chips, CORES), ("dp", "e", "z", "c"))
    expert = ("e", "z", "c")
    tokenwise = P(("dp",) + expert, None)
    in_specs = (tokenwise, tokenwise, tokenwise, P(None, expert), P(None, expert))
    out_specs = (tokenwise, P("dp", expert), P("dp", expert))
    return jax.shard_map(
        device_step, mesh=fine, in_specs=in_specs, out_specs=out_specs, check_vma=False
    )
```

```python
import jax
import jax.numpy as jnp
from jax import lax
from jax.sharding import Mesh, PartitionSpec as P


EXPERTS = 8
TOP = 2
CAP = 4
CORES = 2


def slot_tables(routing_dev):
    flat_experts = routing_dev.reshape(-1)
    onehot = (flat_experts[:, None] == jnp.arange(EXPERTS, dtype=jnp.int32)[None, :]).astype(
        jnp.int32
    )
    before = jnp.cumsum(onehot, axis=0) - onehot
    slot_index = jnp.sum(before * onehot, axis=1)
    target = flat_experts * CAP + slot_index
    placed = target[:, None] == jnp.arange(EXPERTS * CAP, dtype=jnp.int32)[None, :]
    return placed.astype(jnp.float32)


def contract_rows(left_rows, right_rows):
    return lax.dot_general(
        left_rows, right_rows, (((0,), (0,)), ((), ())), preferred_element_type=jnp.float32
    )


def swap_dp(block):
    return lax.ppermute(block, "dp", [(0, 1), (1, 0)])


def swap_core(block):
    return lax.ppermute(block, "c", [(0, 1), (1, 0)])


def ring(block):
    count = lax.axis_size("z")
    route = []
    for at in range(count):
        route.append((at * CORES, (at + 1) % count * CORES))
        route.append((at * CORES + 1, (at - 1) % count * CORES + 1))
    return lax.ppermute(block, ("z", "c"), route)


def device_step(tokens, routing, hidden_grad, gate_weight, up_weight):
    token_count, model_width = tokens.shape
    ffd = gate_weight.shape[1]
    chips = lax.axis_size("z")
    rounds = chips // 2
    half = model_width // 2
    chunk = EXPERTS * CAP
    replica = lax.axis_index("dp")
    core = lax.axis_index("c")
    at = lax.axis_index("z")

    placed = slot_tables(routing)
    chosen = jnp.sum(placed.reshape(token_count, TOP, chunk), axis=1).astype(jnp.bfloat16)
    outgoing = contract_rows(chosen, tokens).astype(jnp.bfloat16)
    mine = lax.all_to_all(
        outgoing.reshape(EXPERTS, CAP, model_width), "e", split_axis=0, concat_axis=0, tiled=True
    ).reshape(chunk, model_width)

    by_chip = hidden_grad.reshape(EXPERTS, chips, CORES, CAP, ffd).transpose(1, 2, 0, 3, 4)
    by_chip = by_chip.reshape(chips, CORES, chunk, ffd)
    by_chip = jnp.where(core == 0, by_chip, by_chip[:, ::-1])
    step = jnp.where(core == 0, -1, 1)

    def grad_rows(k):
        near = lax.dynamic_index_in_dim(by_chip, (at + step * k) % chips, 0, keepdims=False)
        far = lax.dynamic_index_in_dim(by_chip, (at - step * k) % chips, 0, keepdims=False)
        if k == 0:
            return near.reshape(CORES * chunk, ffd)
        if k == rounds - 1:
            across = lax.dynamic_index_in_dim(
                by_chip, (at + rounds) % chips, 0, keepdims=False
            )
            blocks = [near[0], near[1], across[0], far[1], far[0], across[1]]
            return jnp.concatenate(blocks, axis=0)
        return jnp.concatenate([near[0], near[1], far[1], far[0]], axis=0)

    def expert_grads(rows, k):
        grad_h = grad_rows(k).astype(jnp.float32)
        gate_pre = jnp.dot(rows, gate_weight, preferred_element_type=jnp.float32)
        up_pre = jnp.dot(rows, up_weight, preferred_element_type=jnp.float32)
        sig = jax.nn.sigmoid(gate_pre)
        gate_grad = (grad_h * up_pre * sig * (1.0 + gate_pre * (1.0 - sig))).astype(jnp.bfloat16)
        up_grad = (grad_h * gate_pre * sig).astype(jnp.bfloat16)
        return lax.optimization_barrier((gate_grad, up_grad))

    def partial_of(pair):
        transposed = (((1,), (1,)), ((), ()))
        gate_part = lax.dot_general(
            pair[0], gate_weight, transposed, preferred_element_type=jnp.float32
        )
        up_part = lax.dot_general(
            pair[1], up_weight, transposed, preferred_element_type=jnp.float32
        )
        return lax.optimization_barrier((gate_part + up_part).astype(jnp.bfloat16))

    def far_half(blocks):
        block = jnp.concatenate(blocks, axis=0)
        return lax.dynamic_slice_in_dim(block, (1 - replica) * half, half, 1)

    other_mine = swap_core(mine)
    travelling = [mine, other_mine]
    native, other = [mine], [other_mine]
    for k in range(1, rounds + 1):
        moved = []
        for part in travelling if k < rounds else travelling[:1]:
            moved.append(ring(part))
        travelling = (travelling if k == rounds else []) + moved
        if k == rounds - 1:
            third = moved
            continue
        native.append(jnp.concatenate(travelling, axis=0))
        other.append(swap_core(native[-1]))
    sizes = [part.shape[0] for part in native]
    grads = []
    for k in range(rounds):
        block = lax.optimization_barrier(jnp.concatenate([native[k], other[k]], axis=0))
        grads.append(expert_grads(block, k))

    given, kept = {}, {}
    product = partial_of(grads[rounds - 1])
    count = sizes[rounds - 1]
    gift = swap_core(product[:count])
    middle = CORES * chunk
    given[rounds - 1], given[rounds] = gift[:middle], gift[middle:]
    kept[rounds - 1], kept[rounds] = product[count : count + middle], product[count + middle :]
    pair = []
    for which in range(2):
        blocks = [grads[k][which][: sizes[k]] for k in range(rounds - 1)]
        blocks += [grads[k][which][sizes[k] :] for k in range(rounds - 1)]
        pair.append(jnp.concatenate(blocks, axis=0))
    product = partial_of(pair)
    count = sum(sizes[: rounds - 1])
    gift = swap_core(product[chunk:count])
    given[0], kept[0] = product[:chunk], product[count : count + chunk]
    start = chunk
    for k in range(1, rounds - 1):
        given[k] = gift[start - chunk : start - chunk + sizes[k]]
        kept[k] = product[count + start : count + start + sizes[k]]
        start += sizes[k]

    middle = CORES * chunk
    early = swap_dp(far_half(native[: rounds - 1] + [jnp.concatenate(third, axis=0)]))
    early_other = swap_core(early)
    ordered = native[: rounds - 1] + [native[-1][:middle]]
    ordered += other[: rounds - 1] + [other[-1][:middle]]
    ordered += [native[-1][middle:], other[-1][middle:]]
    by_kind = []
    for which in range(2):
        nats = [pair[which][:size] for pair, size in zip(grads, sizes)]
        oths = [pair[which][size:] for pair, size in zip(grads, sizes)]
        blocks = nats[:-1] + [nats[-1][:middle]] + oths[:-1] + [oths[-1][:middle]]
        blocks += [nats[-1][middle:], oths[-1][middle:]]
        by_kind.append(jnp.concatenate(blocks, axis=0))
    own_grads = jnp.concatenate(by_kind, axis=1)
    row_count = own_grads.shape[0]
    last = far_half(ordered[-2:])
    packed = [own_grads] + [last[:, i : i + 2 * ffd] for i in range(0, half, 2 * ffd)]
    received = swap_dp(jnp.concatenate(packed, axis=0))
    far_grads = received[:row_count]
    width = last.shape[0]
    late = [received[i : i + width] for i in range(row_count, received.shape[0], width)]
    far_early = lax.optimization_barrier(jnp.concatenate([early, early_other], axis=0))
    far_rows = jnp.concatenate([far_early, jnp.concatenate(late, axis=1)], axis=0)

    arrived = []
    for k in range(rounds, 0, -1):
        total = []
        for i in range(kept[k].shape[0] // chunk):
            spot = slice(i * chunk, (i + 1) * chunk)
            keep, gift = kept[k][spot], given[k][spot]
            if i > 0:
                keep, gift, total[0] = lax.optimization_barrier((keep, gift, total[0]))
            value = keep.astype(jnp.float32) + gift.astype(jnp.float32)
            if i < len(arrived):
                value = value + arrived[i].astype(jnp.float32)
            total.append(lax.optimization_barrier(value.astype(jnp.bfloat16)))
        arrived = []
        for part in total:
            arrived.append(ring(part))
    arrived = [part.astype(jnp.float32) for part in arrived]
    gift = swap_core((arrived[0] + kept[0].astype(jnp.float32)).astype(jnp.bfloat16))
    summed = gift.astype(jnp.float32) + arrived[1] + given[0].astype(jnp.float32)
    summed = summed.astype(jnp.bfloat16)
    back = lax.all_to_all(
        summed.reshape(EXPERTS, CAP, model_width), "e", split_axis=0, concat_axis=0, tiled=True
    ).reshape(chunk, model_width)
    token_grad = jnp.dot(chosen, back, preferred_element_type=jnp.float32).astype(jnp.bfloat16)

    own_columns = jnp.concatenate(
        [lax.dynamic_slice_in_dim(part, replica * half, half, 1) for part in ordered], axis=0
    )
    own_columns = lax.optimization_barrier(own_columns)
    own_term = contract_rows(own_columns, own_grads).astype(jnp.bfloat16)
    own_term = lax.optimization_barrier(own_term)

    def weight_grad(begin):
        far_term = contract_rows(far_rows, far_grads[:, begin : begin + ffd])
        own_part = own_term[:, begin : begin + ffd].astype(jnp.float32)
        return (own_part + far_term).astype(jnp.bfloat16)

    return (token_grad, weight_grad(0), weight_grad(ffd))


def solution(mesh):
    n_dp, n_expert = mesh.devices.shape
    chips = n_expert // EXPERTS // CORES
    fine = Mesh(mesh.devices.reshape(n_dp, EXPERTS, chips, CORES), ("dp", "e", "z", "c"))
    expert = ("e", "z", "c")
    tokenwise = P(("dp",) + expert, None)
    in_specs = (tokenwise, tokenwise, tokenwise, P(None, expert), P(None, expert))
    out_specs = (tokenwise, P("dp", expert), P("dp", expert))
    return jax.shard_map(
        device_step, mesh=fine, in_specs=in_specs, out_specs=out_specs, check_vma=False
    )
```
